32 devices in a mesh: groups: 2 (over x), segment: 2 (over core), block: 8 (over z, y).
Axes of the slice: x: 2, y: 2, z: 4, core: 2. Of those that a mesh axis runs over, the one named last changes fastest.
Arguments:
- tokens: float32 [1024, 16384], P(('groups', 'segment'), 'block'), parts along dimension 0, may hold values from -32 to 32
- gains: float32 [2, 2, 16384], P('segment', None, 'block'), may hold values from 0.1 to 1.9
- right_factors: float32 [2, 2, 128, 128, 128], P('segment', None, 'block'), may hold values from -0.5 to 0.5
- left_factors: float32 [2, 2, 128, 128, 128], P('segment', None, 'block'), may hold values from -0.5 to 0.5
Outputs:
- output: float32 [1024, 16384], P(('groups', 'segment'), 'block'), parts along dimension 0
The draws below stay inside these ranges and needn't reach their ends.
There are 2 independent parts, one for each index of `groups`. The reference program is written for one: setup_inputs(seed, part) draws one part's arguments, and reference() takes and returns one part's arrays. A program takes and returns all parts, laid end to end along the dimension named above; an argument that names none is the same for every part. Nothing has to cross between parts.
All inputs are finite; a program needn't handle non-finite values.
Results may differ from the reference program's by a relative error of at most 0.0003.
Values sent between devices are 32-bit elements; how exact they have to be, the bound alone decides.
A program may use at most 64 MiB of HBM per device.

```python
import math
import jax
import jax.numpy as jnp
from jax import lax

NB = 128
BS = 128
D = 16384
ROUNDS = 2
TOKENS = 512
N_SEGMENT = 2


def draw_tokens(key, part):
    first_key, second_key = jax.random.split(key, 2)
    position = jnp.arange(D, dtype=jnp.float32) / (D - 1)
    values = jnp.clip(jax.random.normal(first_key, (TOKENS, D), jnp.float32), -5.0, 5.0)
    column_scale = 0.3 * jnp.exp(position * math.log(10.0))
    row_scale = jnp.exp(jax.random.uniform(second_key, (TOKENS, 1), jnp.float32, math.log(0.6), math.log(1.8)))
    return (values * row_scale * column_scale[None, :]).astype(jnp.float32)


def level_of(stream_key, extent, cuts, least, largest):
    loudness = 1.0
    for dim, parts in cuts:
        draws = jax.random.uniform(jax.random.fold_in(jax.random.fold_in(stream_key, 6), dim), (parts,), jnp.float32, least / len(cuts), largest / len(cuts))
        loudness = loudness * jnp.repeat(jnp.exp(draws), extent[dim] // parts).reshape((-1,) + (1,) * (len(extent) - 1 - dim))
    return loudness


def noise(key, extent, width, limit, cuts=(), kind=jnp.bfloat16):
    drawn = width * jax.random.normal(key, extent, jnp.float32)
    if cuts:
        drawn = drawn * level_of(key, extent, cuts, -0.22, 0.18)
    return jnp.clip(drawn, -limit, limit).astype(kind)


def setup_inputs(seed: int = 0, part: int = 0) -> dict:
    splits = jax.random.split(jax.random.key(seed), 5)
    own_keys = jax.random.split(jax.random.fold_in(splits[4], part), 5)
    tokens = draw_tokens(jax.random.fold_in(jax.random.fold_in(splits[4], part), 71), part)
    gains = jnp.clip(1.0 + 0.18 * jax.random.normal(splits[1], (N_SEGMENT, ROUNDS, D), jnp.float32), 0.1, 1.9)
    right_factors = noise(splits[2], (N_SEGMENT, ROUNDS, NB, BS, BS), BS ** -0.5, 0.5, ((0, 2), (2, 8)), jnp.float32)
    left_factors = noise(splits[3], (N_SEGMENT, ROUNDS, BS, NB, NB), NB ** -0.5, 0.5, ((0, 2), (2, 8)), jnp.float32)
    return {"tokens": tokens, "gains": gains, "right_factors": right_factors, "left_factors": left_factors}


epsilon = 1e-06

def one_layer(current, gain_row, right_part, left_part):
    sum_squares = lax.optimization_barrier(jnp.sum(current * current, axis=1, keepdims=True))
    normed = current * lax.rsqrt(sum_squares / D + epsilon) * gain_row[None, :]
    inner = jnp.einsum('tbi,bij->tbj', normed.reshape(-1, NB, BS), right_part, precision=lax.Precision.HIGHEST)
    mixed = jnp.einsum('tbj,jbc->tcj', inner, left_part, precision=lax.Precision.HIGHEST)
    return current + mixed.reshape(-1, D) * jax.nn.silu(normed)

def reference(tokens, gains, right_factors, left_factors):
    current = tokens
    for round_number in range(ROUNDS):
        for section in range(N_SEGMENT):
            current = one_layer(current, gains[section, round_number], right_factors[section, round_number], left_factors[section, round_number])
    return current
```

```python
import functools

import jax
import jax.numpy as jnp
from jax import lax
from jax.experimental import pallas as pl
from jax.experimental.pallas import tpu as pltpu
from jax.sharding import Mesh, PartitionSpec as P

D = 16384


epsilon = 1e-06
exact = lax.Precision.HIGH


def shifted(block, axis, distance):
    devices = range(lax.axis_size(axis))
    route = [((i - distance) % len(devices), i) for i in devices]
    return lax.ppermute(block, axis, route)


def apply_layer(current, gain_row, right_part, left_part):
    blocks_here = right_part.shape[0]
    block_size = right_part.shape[1]
    width_here, token_count = current.shape
    partial_squares = jnp.sum(current * current, axis=0)
    devices = lax.axis_size("block")
    copies = jnp.broadcast_to(partial_squares, (devices, token_count))
    sum_squares = lax.all_to_all(copies, "block", 0, 0, tiled=True).sum(axis=0)
    normed = current * lax.rsqrt(sum_squares / D + epsilon)[None, :] * gain_row[:, None]
    inner = jnp.einsum(
        "bit,bij->bjt",
        normed.reshape(blocks_here, block_size, token_count),
        right_part,
        precision=exact,
    )
    combined = jnp.einsum(
        "bjt,jbc->cjt",
        lax.all_to_all(inner, "block", split_axis=1, concat_axis=0, tiled=True),
        left_part,
        precision=exact,
    )
    mixed = lax.all_to_all(combined, "block", split_axis=0, concat_axis=1, tiled=True)
    return current + mixed.reshape(width_here, token_count) * jax.nn.silu(normed)


def body(tokens, gains, right_factors, left_factors):
    current = tokens.T
    rounds = right_factors.shape[1]
    segment_index = lax.axis_index("segment")
    own = (gains[0], right_factors[0], left_factors[0])
    other = [[shifted(part[r], "segment", 1) for part in own] for r in range(rounds)]
    for layer_index in range(2 * rounds):
        section, r = layer_index % 2, layer_index // 2
        chosen = [
            jnp.where(segment_index == section, mine[r], theirs)
            for mine, theirs in zip(own, other[r])
        ]
        current = apply_layer(current, *chosen)
    return current.T


MESH = pl.DeviceIdType.MESH


def halves(value):
    high = value.astype(jnp.bfloat16)
    return high, (value - high.astype(jnp.float32)).astype(jnp.bfloat16)


def product(weight, value):
    wh, wl = halves(weight)
    vh, vl = halves(value)
    dot = functools.partial(jnp.dot, preferred_element_type=jnp.float32)
    return dot(wh, vh) + (dot(wh, vl) + dot(wl, vh))


def layers_kernel(
    hi, layers, token_ref, gain_ref, right_ref, left_ref, out_ref,
    W, X, N, S, A, T, M, Q, B, G, P,
    tsend, trecv, gsend, grecv, osend, orecv,
    wsend, wrecv, rsend, fsend, frecv, qsend, qrecv, asend, arecv, msend, mrecv,
):
    x = lax.axis_index("groups")
    c = lax.axis_index("segment")
    z = lax.axis_index("hi")
    y = lax.axis_index("lo")
    here = 2 * y + c
    half = W.shape[2] // 2
    own = pl.ds(pl.multiple_of(x * half, half), half)
    steps = 2 * layers
    beside = z + 1 - 2 * (z % 2)
    across = 2 - z // 2
    far = 2 - 2 * (z // 2)
    inner_plane = (z == 1) | (z == 2)
    planes = (z, beside, far, far + 1)
    few, wide = B.shape[2] // 2, B.shape[3]
    low = lax.broadcasted_iota(jnp.int32, (128, 128), 1) < 64

    def peer(d):
        return (x, (c + d % 2) % 2, z, (y + d // 2) % 2)

    G[...] = jnp.zeros(G.shape, jnp.float32)
    barrier = pltpu.get_barrier_semaphore()
    greeted = [(x, (c + dc) % 2, (z + dz) % hi, y) for dz in range(hi) for dc in range(2) if dz or dc]
    greeted += [peer(2), peer(3), (1 - x, c, z, y)]
    for device in greeted:
        pl.semaphore_signal(barrier, inc=1, device_id=device, device_id_type=MESH)
    pl.semaphore_wait(barrier, len(greeted))

    def copy_to(src, dst, send, recv, i, dc):
        if i == 0 and dc == 0:
            return pltpu.make_async_copy(src, dst, recv)
        return pltpu.make_async_remote_copy(
            src_ref=src, dst_ref=dst, send_sem=send, recv_sem=recv,
            device_id=(x, (c + dc) % 2, planes[i], y), device_id_type=MESH,
        )

    others = [(i, dc) for i in range(4) for dc in range(2)]

    def token_copy(h, i, dc):
        rows = pl.ds(pl.multiple_of((2 * planes[i] + h) * few, few), few)
        columns = pl.ds(pl.multiple_of((c + dc) % 2 * wide, wide), wide)
        dst = B.at[h, z, pl.ds(pl.multiple_of(c * few, few), few)]
        return copy_to(token_ref.at[rows, columns], dst, tsend.at[h, i, dc], trecv.at[h, z, c], i, dc)

    def gain_copy(i, dc):
        src = gain_ref.at[:, (c + dc) % 2]
        dst = G.at[c, :, pl.ds(pl.multiple_of(z * 8, 8), 8)]
        return copy_to(src, dst, gsend.at[i, dc], grecv.at[z, c], i, dc)

    def out_copy(h, i, dc):
        src = B.at[h, planes[i], pl.ds(pl.multiple_of((c + dc) % 2 * few, few), few)]
        rows = pl.ds(pl.multiple_of((2 * z + h) * few, few), few)
        columns = pl.ds(pl.multiple_of(c * wide, wide), wide)
        return copy_to(src, out_ref.at[rows, columns], osend.at[h, i, dc], orecv.at[h, z, c], i, dc)

    def push_copies(step, f):
        r = step // 4
        source = (right_ref, left_ref)[f]
        send = wsend.at[r * 2 + f]
        for dc in range(2):
            rows = pl.ds(pl.multiple_of((c + dc) % 2 * 2 * half, 2 * half), 2 * half)
            yield copy_to(source.at[r, rows], W.at[step, z], send.at[dc], wrecv.at[step, z], 0, dc)
        for i, plane in enumerate((beside, across)):
            for dc in range(2):
                rows = pl.ds(pl.multiple_of(((c + dc) % 2 * 2 + x) * half, half), half)
                yield pltpu.make_async_remote_copy(
                    src_ref=source.at[r, rows], dst_ref=W.at[step, z, own],
                    send_sem=send.at[2 + 2 * i + dc], recv_sem=wrecv.at[step, z],
                    device_id=(x, (c + dc) % 2, plane, y), device_id_type=MESH,
                )

    def push(step, f):
        @pl.when(c == (step // 2) % 2)
        def _():
            for copy in push_copies(step, f):
                copy.start()

    def forward_copy(step, plane):
        piece = W.at[step, plane, own]
        return pltpu.make_async_remote_copy(
            src_ref=piece, dst_ref=piece, send_sem=fsend.at[step, plane], recv_sem=frecv.at[step, plane],
            device_id=(1 - x, c, z, y), device_id_type=MESH,
        )

    def relay_copy(step, i):
        piece = W.at[step, far + i, own]
        return pltpu.make_async_remote_copy(
            src_ref=piece, dst_ref=piece, send_sem=rsend.at[step, i], recv_sem=wrecv.at[step, far + i],
            device_id=(x, c, beside, y), device_id_type=MESH,
        )

    def piece_wait(step, plane):
        piece = W.at[step, plane, own]
        pltpu.make_async_copy(piece, piece, wrecv.at[step, plane]).wait()

    def spread(step):
        piece_wait(step, beside)
        forward_copy(step, beside).start()

        @pl.when(inner_plane)
        def _():
            for i in range(2):
                piece_wait(step, far + i)
                relay_copy(step, i).start()
                forward_copy(step, far + i).start()

    def spread_relayed(step):
        @pl.when(~inner_plane)
        def _():
            for i in range(2):
                piece_wait(step, far + i)
                forward_copy(step, far + i).start()

    def arrived_near(step):
        pltpu.make_async_copy(W.at[step, z], W.at[step, z], wrecv.at[step, z]).wait()
        forward_copy(step, beside).wait_recv()

    def arrived_far(step):
        for i in range(2):
            forward_copy(step, far + i).wait_recv()

    def quad_copy(kind, h, part, d):
        if kind == "q":
            ref = Q.at[part, h, here]
            src, dst, send, recv = ref, ref, qsend.at[part, h, d], qrecv.at[part, h, d]
        else:
            target = 2 * ((y + d // 2) % 2) + (c + d % 2) % 2
            if kind == "a":
                src, dst, send, recv = S.at[h, part, target], A.at[h, :, part, here], asend, arecv
            else:
                src, dst, send, recv = T.at[h, part, target], M.at[h, part, here], msend, mrecv
            send, recv = send.at[h, part, d], recv.at[h, part, d]
            if d == 0:
                return pltpu.make_async_copy(src, dst, recv)
        return pltpu.make_async_remote_copy(
            src_ref=src, dst_ref=dst, send_sem=send, recv_sem=recv,
            device_id=peer(d), device_id_type=MESH,
        )

    def squares(value):
        return jnp.sum((value * value).reshape(16, 8, 128), axis=0)

    def right_pair(l, h, u, k, value):
        p = u * 8 + k
        v = value * P[l, p]
        N[h, p] = v
        packed = jnp.concatenate([jnp.where(low, v, 0.0), jnp.where(low, 0.0, v)], axis=0)
        weight = jnp.concatenate([W[2 * l, 2 * u + e, k * 128:(k + 1) * 128] for e in range(2)], axis=1)
        tiles = product(weight, packed).reshape(hi, 4, 8, 128)
        for q in range(4):
            S[h, u, q, :, k] = tiles[:, q]

    def send_inner(h, u):
        for d in (2, 3, 1, 0):
            quad_copy("a", h, u, d).start()

    def send_squares(l, h, total):
        Q[l, h, here] = total
        for d in (2, 3, 1):
            quad_copy("q", h, l, d).start()

    def first_part(h, u):
        total = jnp.zeros((8, 128), jnp.float32)
        for e in range(2):
            for cc in range(2):
                piece = B.at[h, 2 * u + e, :few]
                pltpu.make_async_copy(piece, piece, trecv.at[h, 2 * u + e, cc]).wait()
        for k in range(8):
            columns = slice(k * 128, (k + 1) * 128)
            value = jnp.concatenate([B[h, 2 * u, :, columns], B[h, 2 * u + 1, :, columns]], axis=0).T
            X[h, u * 8 + k] = value
            right_pair(0, h, u, k, value)
            total = total + squares(value)
        send_inner(h, u)
        return total

    def left_stage(l, h):
        for part in range(2):
            for d in range(4):
                quad_copy("a", h, part, d).wait()

        def left_chunk(zj, carry):
            flat = A.at[h, zj].reshape(2 * 4 * 8 * 8, 128)
            for jj in range(8):
                a = flat[pl.ds(jj, 64, stride=8), :]
                swapped = pltpu.roll(a, 64, 1)
                mask = low[:64]
                al, ah = jnp.where(mask, a, 0.0), jnp.where(mask, 0.0, a)
                sl, sh = jnp.where(mask, swapped, 0.0), jnp.where(mask, 0.0, swapped)
                packed = jnp.concatenate(
                    [al[:32], sl[:32], al[32:], sl[32:], sh[:32], ah[:32], sh[32:], ah[32:]], axis=0
                )
                w = W[2 * l + 1, zj, jj * 128:(jj + 1) * 128]
                weight = jnp.concatenate(
                    [jnp.concatenate([w[s:s + 32], w[s + 64:s + 96]], axis=0) for s in (0, 32)], axis=1
                )
                tiles = product(weight, packed).reshape(2, 4, 8, 128)
                for q in range(4):
                    T[h, zj, q, jj] = tiles[:, q]
            for d in (2, 3, 1, 0):
                quad_copy("m", h, zj, d).start()
            return carry

        lax.fori_loop(0, hi, left_chunk, 0)

    def closing(l, h):
        for d in (2, 3, 1):
            quad_copy("q", h, l, d).wait()
        everyone = Q[l, h, 0] + Q[l, h, 1] + Q[l, h, 2] + Q[l, h, 3]
        one = jnp.sum(everyone, axis=0, keepdims=True)
        both = jnp.broadcast_to(one, (8, 128))
        both = both + pltpu.roll(both, 64, 1)
        scale = lax.rsqrt(both[:1] / D + epsilon)
        for part in range(hi):
            for d in range(4):
                quad_copy("m", h, part, d).wait()
        flat = M.at[h].reshape(128 * 16, 128)

        def close_pair(p):
            normed = N[h, p] * scale
            mixed = flat[pl.ds(p, 128, stride=16), :] * scale
            return X[h, p] + mixed * (normed / (1.0 + jnp.exp(-normed)))

        return close_pair

    def next_stage(l, h):
        close_pair = closing(l, h)

        def part(u, total):
            for k in range(8):
                value = close_pair(u * 8 + k)
                X[h, u * 8 + k] = value
                right_pair(l + 1, h, u, k, value)
                total = total + squares(value)
            send_inner(h, u)
            return total

        send_squares(l + 1, h, lax.fori_loop(0, 2, part, jnp.zeros((8, 128), jnp.float32)))

    def last_stage(l, h):
        close_pair = closing(l, h)
        for near in (0, 1):
            u = (z // 2 + 1 - near) % 2
            for k in range(8):
                columns = slice(k * 128, (k + 1) * 128)
                value = close_pair(u * 8 + k).T
                B[h, 2 * u, :, columns] = value[:2 * few]
                B[h, 2 * u + 1, :, columns] = value[2 * few:]
            for i in ((2, 3), (1, 0))[near]:
                for dc in range(2):
                    out_copy(h, i, dc).start()

    for i, dc in others:
        gain_copy(i, dc).start()
    push(0, 0)
    for i, dc in others:
        token_copy(0, i, dc).start()
    for zz in range(hi):
        for cc in range(2):
            piece = G.at[cc, :, zz * 8:(zz + 1) * 8]
            pltpu.make_async_copy(piece, piece, grecv.at[zz, cc]).wait()

    def pack_gains(l, carry):
        columns = G[l % 2, l // 2].T
        for u in range(2):
            for k in range(8):
                first, second = u * 16 + k, u * 16 + 8 + k
                P[l, u * 8 + k] = jnp.where(low, columns[:, first:first + 1], columns[:, second:second + 1])
        return carry

    lax.fori_loop(0, layers, pack_gains, 0)
    near_u, far_u = z // 2, 1 - z // 2
    spread(0)
    for i, dc in others:
        token_copy(1, i, dc).start()
    arrived_near(0)
    total = first_part(0, near_u)
    spread_relayed(0)
    push(1, 1)
    arrived_far(0)
    total = total + first_part(0, far_u)
    send_squares(0, 0, total)
    total = first_part(1, near_u)
    total = total + first_part(1, far_u)
    send_squares(0, 1, total)
    spread(1)
    push(2, 0)
    spread_relayed(1)
    spread(2)
    push(3, 1)
    arrived_near(1)
    arrived_far(1)

    def layer(l, carry):
        left_stage(l, 0)
        left_stage(l, 1)
        spread_relayed(2 * l + 2)

        spread(2 * l + 3)

        @pl.when(2 * l + 4 < steps)
        def _():
            push(2 * l + 4, 0)

        arrived_near(2 * l + 2)
        arrived_far(2 * l + 2)
        next_stage(l, 0)
        next_stage(l, 1)
        spread_relayed(2 * l + 3)

        @pl.when(2 * l + 4 < steps)
        def _():
            spread(2 * l + 4)
            push(2 * l + 5, 1)

        arrived_near(2 * l + 3)
        arrived_far(2 * l + 3)
        return carry

    lax.fori_loop(0, layers - 1, layer, 0)
    left_stage(layers - 1, 0)
    left_stage(layers - 1, 1)
    last_stage(layers - 1, 0)
    last_stage(layers - 1, 1)

    for step in range(steps):
        @pl.when(c == (step // 2) % 2)
        def _():
            for i, copy in enumerate(push_copies(step, step % 2)):
                if i:
                    copy.wait_send()

        for i in range(1, 4):
            forward_copy(step, planes[i]).wait_send()

        @pl.when(inner_plane)
        def _():
            for i in range(2):
                relay_copy(step, i).wait_send()

    for i, dc in others:
        if i or dc:
            gain_copy(i, dc).wait_send()
            for h in range(2):
                token_copy(h, i, dc).wait_send()
                out_copy(h, i, dc).wait_send()
    for h in range(2):
        for zz in range(hi):
            for cc in range(2):
                first = (2 * zz + h) * few
                piece = out_ref.at[first:first + few, cc * wide:(cc + 1) * wide]
                pltpu.make_async_copy(piece, piece, orecv.at[h, zz, cc]).wait()


def quad_body(tokens, gains, right_factors, left_factors):
    f32 = jnp.float32
    hi = lax.axis_size("hi")
    rounds, here, size = right_factors.shape[1:4]
    layers = 2 * rounds
    rows = here * size // 2
    few = tokens.shape[0] // hi
    rates = gains[0].reshape(rounds, 2, here // 2, size)
    rights = right_factors[0].swapaxes(-1, -2).reshape(rounds, here * size, size)
    lefts = left_factors[0].swapaxes(-1, -2).reshape(rounds, here * size, size)
    dma = pltpu.SemaphoreType.DMA
    anywhere = pl.BlockSpec(memory_space=pl.ANY)
    return pl.pallas_call(
        functools.partial(layers_kernel, hi, layers),
        out_shape=jax.ShapeDtypeStruct(tokens.shape, f32),
        in_specs=[anywhere] * 4,
        out_specs=anywhere,
        scratch_shapes=[
            pltpu.VMEM((2 * layers, hi, rows, 128), f32),
            pltpu.VMEM((2, hi * 4, 128, 128), f32),
            pltpu.VMEM((2, hi * 4, 128, 128), f32),
            pltpu.VMEM((2, 2, 4, hi, 8, 8, 128), f32),
            pltpu.VMEM((2, hi, 2, 4, 8, 8, 128), f32),
            pltpu.VMEM((2, hi, 4, 8, 2, 8, 128), f32),
            pltpu.VMEM((2, hi, 4, 8, 2, 8, 128), f32),
            pltpu.VMEM((layers, 2, 4, 8, 128), f32),
            pltpu.VMEM((2, hi, few, rows), f32),
            pltpu.VMEM((2, rounds, 128, 128), f32),
            pltpu.VMEM((layers, hi * 4, 128, 128), f32),
            dma((2, hi, 2)),
            dma((2, hi, 2)),
            dma((hi, 2)),
            dma((hi, 2)),
            dma((2, hi, 2)),
            dma((2, hi, 2)),
            dma((layers, 6)),
            dma((2 * layers, hi)),
            dma((2 * layers, 2)),
            dma((2 * layers, hi)),
            dma((2 * layers, hi)),
            dma((layers, 2, 4)),
            dma((layers, 2, 4)),
            dma((2, 2, 4)),
            dma((2, 2, 4)),
            dma((2, hi, 4)),
            dma((2, hi, 4)),
        ],
        compiler_params=pltpu.CompilerParams(
            collective_id=0, has_side_effects=True, vmem_limit_bytes=58 * 2**20
        ),
    )(tokens, rates, rights, lefts)


def solution(mesh):
    groups, segments, devices = (mesh.shape[a] for a in ("groups", "segment", "block"))
    if (groups, segments, devices) == (2, 2, 8):
        finer = Mesh(mesh.devices.reshape(2, 2, 4, 2), ("groups", "segment", "hi", "lo"))
        block, chosen = ("hi", "lo"), quad_body
    else:
        finer, block, chosen = mesh, "block", body
    placed = (
        P(("groups", "segment"), block),
        P("segment", None, block),
        P("segment", None, block, None, None),
        P("segment", None, block, None, None),
    )
    return jax.shard_map(
        chosen,
        mesh=finer,
        in_specs=placed,
        out_specs=P(("groups", "segment"), block),
        check_vma=False,
    )
```

```python
import functools

import jax
import jax.numpy as jnp
from jax import lax
from jax.experimental import pallas as pl
from jax.experimental.pallas import tpu as pltpu
from jax.sharding import Mesh, PartitionSpec as P

D = 16384


epsilon = 1e-06
exact = lax.Precision.HIGH


def shifted(block, axis, distance):
    devices = range(lax.axis_size(axis))
    route = [((i - distance) % len(devices), i) for i in devices]
    return lax.ppermute(block, axis, route)


def apply_layer(current, gain_row, right_part, left_part):
    blocks_here = right_part.shape[0]
    block_size = right_part.shape[1]
    width_here, token_count = current.shape
    partial_squares = jnp.sum(current * current, axis=0)
    devices = lax.axis_size("block")
    copies = jnp.broadcast_to(partial_squares, (devices, token_count))
    sum_squares = lax.all_to_all(copies, "block", 0, 0, tiled=True).sum(axis=0)
    normed = current * lax.rsqrt(sum_squares / D + epsilon)[None, :] * gain_row[:, None]
    inner = jnp.einsum(
        "bit,bij->bjt",
        normed.reshape(blocks_here, block_size, token_count),
        right_part,
        precision=exact,
    )
    combined = jnp.einsum(
        "bjt,jbc->cjt",
        lax.all_to_all(inner, "block", split_axis=1, concat_axis=0, tiled=True),
        left_part,
        precision=exact,
    )
    mixed = lax.all_to_all(combined, "block", split_axis=0, concat_axis=1, tiled=True)
    return current + mixed.reshape(width_here, token_count) * jax.nn.silu(normed)


def body(tokens, gains, right_factors, left_factors):
    current = tokens.T
    rounds = right_factors.shape[1]
    segment_index = lax.axis_index("segment")
    own = (gains[0], right_factors[0], left_factors[0])
    other = [[shifted(part[r], "segment", 1) for part in own] for r in range(rounds)]
    for layer_index in range(2 * rounds):
        section, r = layer_index % 2, layer_index // 2
        chosen = [
            jnp.where(segment_index == section, mine[r], theirs)
            for mine, theirs in zip(own, other[r])
        ]
        current = apply_layer(current, *chosen)
    return current.T


MESH = pl.DeviceIdType.MESH


def halves(value):
    high = value.astype(jnp.bfloat16)
    return high, (value - high.astype(jnp.float32)).astype(jnp.bfloat16)


def product(weight, value):
    wh, wl = halves(weight)
    vh, vl = halves(value)
    dot = functools.partial(jnp.dot, preferred_element_type=jnp.float32)
    return dot(wh, vh) + (dot(wh, vl) + dot(wl, vh))


def layers_kernel(
    hi, layers, token_ref, gain_ref, right_ref, left_ref, out_ref,
    W, X, N, S, A, T, M, Q, B, G, P,
    tsend, trecv, gsend, grecv, osend, orecv,
    ssend, psend, wrecv, rsend, fsend, frecv, qsend, qrecv, asend, arecv, msend, mrecv, nsend, nrecv,
):
    x = lax.axis_index("groups")
    c = lax.axis_index("segment")
    z = lax.axis_index("hi")
    y = lax.axis_index("lo")
    here = 2 * y + c
    half = W.shape[2] // 2
    cuts = psend.shape[2]
    steps = 2 * layers
    beside = z + 1 - 2 * (z % 2)
    across = 2 - z // 2
    far = 2 - 2 * (z // 2)
    inner_plane = (z == 1) | (z == 2)
    planes = (z, beside, far, far + 1)
    few, wide = B.shape[2] // 2, B.shape[3]
    near_u, far_u = z // 2, 1 - z // 2
    low = lax.broadcasted_iota(jnp.int32, (128, 128), 1) < 64

    def peer(d):
        return (x, (c + d % 2) % 2, z, (y + d // 2) % 2)

    G[...] = jnp.zeros(G.shape, jnp.float32)
    barrier = pltpu.get_barrier_semaphore()
    greeted = [(x, (c + dc) % 2, (z + dz) % hi, y) for dz in range(hi) for dc in range(2) if dz or dc]
    greeted += [peer(2), peer(3), (1 - x, c, z, y)]
    for device in greeted:
        pl.semaphore_signal(barrier, inc=1, device_id=device, device_id_type=MESH)
    pl.semaphore_wait(barrier, len(greeted))

    def copy_to(src, dst, send, recv, i, dc):
        if i == 0 and dc == 0:
            return pltpu.make_async_copy(src, dst, recv)
        return pltpu.make_async_remote_copy(
            src_ref=src, dst_ref=dst, send_sem=send, recv_sem=recv,
            device_id=(x, (c + dc) % 2, planes[i], y), device_id_type=MESH,
        )

    others = [(i, dc) for i in range(4) for dc in range(2)]

    def token_copy(h, i, dc):
        rows = pl.ds(pl.multiple_of((2 * planes[i] + h) * few, few), few)
        columns = pl.ds(pl.multiple_of((c + dc) % 2 * wide, wide), wide)
        dst = B.at[h, z, pl.ds(pl.multiple_of(c * few, few), few)]
        return copy_to(token_ref.at[rows, columns], dst, tsend.at[h, i, dc], trecv.at[h, z, c], i, dc)

    def gain_copy(i, dc):
        src = gain_ref.at[:, (c + dc) % 2]
        dst = G.at[c, :, pl.ds(pl.multiple_of(z * 8, 8), 8)]
        return copy_to(src, dst, gsend.at[i, dc], grecv.at[z, c], i, dc)

    def out_copy(h, i, dc):
        src = B.at[h, planes[i], pl.ds(pl.multiple_of((c + dc) % 2 * few, few), few)]
        rows = pl.ds(pl.multiple_of((2 * z + h) * few, few), few)
        columns = pl.ds(pl.multiple_of(c * wide, wide), wide)
        return copy_to(src, out_ref.at[rows, columns], osend.at[h, i, dc], orecv.at[h, z, c], i, dc)

    def share_copy(step, f, dc):
        source = (right_ref, left_ref)[f]
        rows = pl.ds(pl.multiple_of((c + dc) % 2 * 2 * half, 2 * half), 2 * half)
        src = source.at[step // 4, rows]
        return copy_to(src, W.at[step, z], ssend.at[step], wrecv.at[step, z, 0], 0, dc)

    def share(step, f):
        @pl.when(c == (step // 2) % 2)
        def _():
            for dc in (1, 0):
                share_copy(step, f, dc).start()

    def piece_at(step, plane, s):
        size = half // cuts
        return W.at[step, plane, pl.ds(pl.multiple_of(x * half + s * size, size), size)]

    def push_copy(step, i, s):
        piece = piece_at(step, z, s)
        return pltpu.make_async_remote_copy(
            src_ref=piece, dst_ref=piece, send_sem=psend.at[step, i, s], recv_sem=wrecv.at[step, z, s],
            device_id=(x, c, (across, beside)[i], y), device_id_type=MESH,
        )

    def push(step):
        pltpu.make_async_copy(W.at[step, z], W.at[step, z], wrecv.at[step, z, 0]).wait()
        for s in range(cuts):
            for i in range(2):
                push_copy(step, i, s).start()

    def forward_copy(step, plane, s):
        piece = piece_at(step, plane, s)
        return pltpu.make_async_remote_copy(
            src_ref=piece, dst_ref=piece,
            send_sem=fsend.at[step, plane, s], recv_sem=frecv.at[step, plane, s],
            device_id=(1 - x, c, z, y), device_id_type=MESH,
        )

    def relay_copy(step, i, s):
        piece = piece_at(step, far + i, s)
        return pltpu.make_async_remote_copy(
            src_ref=piece, dst_ref=piece,
            send_sem=rsend.at[step, i, s], recv_sem=wrecv.at[step, far + i, s],
            device_id=(x, c, beside, y), device_id_type=MESH,
        )

    def piece_wait(step, plane, s):
        piece = piece_at(step, plane, s)
        pltpu.make_async_copy(piece, piece, wrecv.at[step, plane, s]).wait()

    def spread(step):
        for s in range(cuts):
            piece_wait(step, beside, s)
            forward_copy(step, beside, s).start()

            @pl.when(inner_plane)
            def _():
                for i in range(2):
                    piece_wait(step, far + i, s)
                    relay_copy(step, i, s).start()
                    forward_copy(step, far + i, s).start()

    def spread_relayed(step):
        @pl.when(~inner_plane)
        def _():
            for s in range(cuts):
                for i in range(2):
                    piece_wait(step, far + i, s)
                    forward_copy(step, far + i, s).start()

    def arrived_near(step):
        for s in range(cuts):
            forward_copy(step, beside, s).wait_recv()

    def arrived_far(step):
        for s in range(cuts):
            for i in range(2):
                forward_copy(step, far + i, s).wait_recv()

    def arrived(step):
        arrived_near(step)
        arrived_far(step)

    def quad_copy(kind, h, part, d):
        if kind == "q":
            ref = Q.at[part, h, here]
            src, dst, send, recv = ref, ref, qsend.at[part, h, d], qrecv.at[part, h, d]
        else:
            target = 2 * ((y + d // 2) % 2) + (c + d % 2) % 2
            if kind == "a":
                src, dst, send, recv = S.at[h, part, target], A.at[h, :, part, here], asend, arecv
            elif kind == "m":
                src, dst, send, recv = T.at[h, part, target], M.at[h, part, here], msend, mrecv
            else:
                src, dst, send, recv = T.at[h, :, target, :, part], M.at[h, :, here, :, part], nsend, nrecv
            send, recv = send.at[h, part, d], recv.at[h, part, d]
            if d == 0:
                return pltpu.make_async_copy(src, dst, recv)
        return pltpu.make_async_remote_copy(
            src_ref=src, dst_ref=dst, send_sem=send, recv_sem=recv,
            device_id=peer(d), device_id_type=MESH,
        )

    def squares(value):
        return jnp.sum((value * value).reshape(16, 8, 128), axis=0)

    def right_pair(l, h, u, k, value):
        p = u * 8 + k
        v = value * P[l, p]
        N[h, p] = v
        packed = jnp.concatenate([jnp.where(low, v, 0.0), jnp.where(low, 0.0, v)], axis=0)
        weight = jnp.concatenate([W[2 * l, 2 * u + e, k * 128:(k + 1) * 128] for e in range(2)], axis=1)
        tiles = product(weight, packed).reshape(hi, 4, 8, 128)
        for q in range(4):
            S[h, u, q, :, k] = tiles[:, q]

    def send_inner(h, u):
        for d in (2, 3, 1, 0):
            quad_copy("a", h, u, d).start()

    def send_squares(l, h, total):
        Q[l, h, here] = total
        for d in (2, 3, 1):
            quad_copy("q", h, l, d).start()

    def first_part(h, u):
        total = jnp.zeros((8, 128), jnp.float32)
        for e in range(2):
            for cc in range(2):
                piece = B.at[h, 2 * u + e, :few]
                pltpu.make_async_copy(piece, piece, trecv.at[h, 2 * u + e, cc]).wait()
        for k in range(8):
            columns = slice(k * 128, (k + 1) * 128)
            value = jnp.concatenate([B[h, 2 * u, :, columns], B[h, 2 * u + 1, :, columns]], axis=0).T
            X[h, u * 8 + k] = value
            right_pair(0, h, u, k, value)
            total = total + squares(value)
        send_inner(h, u)
        return total

    def left_stage(l, h, last=False):
        for part in range(2):
            for d in range(4):
                quad_copy("a", h, part, d).wait()

        def left_chunk(zj, carry):
            flat = A.at[h, zj].reshape(2 * 4 * 8 * 8, 128)
            for jj in range(8):
                a = flat[pl.ds(jj, 64, stride=8), :]
                swapped = pltpu.roll(a, 64, 1)
                mask = low[:64]
                al, ah = jnp.where(mask, a, 0.0), jnp.where(mask, 0.0, a)
                sl, sh = jnp.where(mask, swapped, 0.0), jnp.where(mask, 0.0, swapped)
                packed = jnp.concatenate(
                    [al[:32], sl[:32], al[32:], sl[32:], sh[:32], ah[:32], sh[32:], ah[32:]], axis=0
                )
                w = W[2 * l + 1, zj, jj * 128:(jj + 1) * 128]
                weight = jnp.concatenate(
                    [jnp.concatenate([w[s:s + 32], w[s + 64:s + 96]], axis=0) for s in (0, 32)], axis=1
                )
                tiles = product(weight, packed).reshape(2, 4, 8, 128)
                for q in range(4):
                    T[h, zj, q, jj] = tiles[:, q]
            if not last:
                for d in (2, 3, 1, 0):
                    quad_copy("m", h, zj, d).start()
            return carry

        lax.fori_loop(0, hi, left_chunk, 0)
        if last:
            for u in (far_u, near_u):
                for d in (2, 3, 1, 0):
                    quad_copy("n", h, u, d).start()

    def closing(l, h):
        for d in (2, 3, 1):
            quad_copy("q", h, l, d).wait()
        everyone = Q[l, h, 0] + Q[l, h, 1] + Q[l, h, 2] + Q[l, h, 3]
        one = jnp.sum(everyone, axis=0, keepdims=True)
        both = jnp.broadcast_to(one, (8, 128))
        both = both + pltpu.roll(both, 64, 1)
        scale = lax.rsqrt(both[:1] / D + epsilon)
        flat = M.at[h].reshape(128 * 16, 128)

        def close_pair(p):
            normed = N[h, p] * scale
            mixed = flat[pl.ds(p, 128, stride=16), :] * scale
            return X[h, p] + mixed * (normed / (1.0 + jnp.exp(-normed)))

        return close_pair

    def next_stage(l, h):
        close_pair = closing(l, h)
        for part in range(hi):
            for d in range(4):
                quad_copy("m", h, part, d).wait()

        def part(u, total):
            for k in range(8):
                value = close_pair(u * 8 + k)
                X[h, u * 8 + k] = value
                right_pair(l + 1, h, u, k, value)
                total = total + squares(value)
            send_inner(h, u)
            return total

        send_squares(l + 1, h, lax.fori_loop(0, 2, part, jnp.zeros((8, 128), jnp.float32)))

    def last_stage(l, h):
        close_pair = closing(l, h)
        for near in (0, 1):
            u = (far_u, near_u)[near]
            for d in range(4):
                quad_copy("n", h, u, d).wait()
            for k in range(8):
                columns = slice(k * 128, (k + 1) * 128)
                value = close_pair(u * 8 + k).T
                B[h, 2 * u, :, columns] = value[:2 * few]
                B[h, 2 * u + 1, :, columns] = value[2 * few:]
            for i in ((2, 3), (1, 0))[near]:
                for dc in range(2):
                    out_copy(h, i, dc).start()

    for i, dc in others:
        gain_copy(i, dc).start()
    for step in range(4):
        share(step, step % 2)
    for i, dc in others[:4]:
        token_copy(0, i, dc).start()
    push(0)
    push(1)
    for i, dc in others[4:]:
        token_copy(0, i, dc).start()
    for step in range(4, steps):
        share(step, step % 2)
    for zz in range(hi):
        for cc in range(2):
            piece = G.at[cc, :, zz * 8:(zz + 1) * 8]
            pltpu.make_async_copy(piece, piece, grecv.at[zz, cc]).wait()

    def pack_gains(l, carry):
        columns = G[l % 2, l // 2].T
        for u in range(2):
            for k in range(8):
                first, second = u * 16 + k, u * 16 + 8 + k
                P[l, u * 8 + k] = jnp.where(low, columns[:, first:first + 1], columns[:, second:second + 1])
        return carry

    lax.fori_loop(0, layers, pack_gains, 0)
    spread(0)
    spread(1)
    for i, dc in others:
        token_copy(1, i, dc).start()
    push(2)
    arrived_near(0)
    total = first_part(0, near_u)
    spread_relayed(0)
    arrived_far(0)
    total = total + first_part(0, far_u)
    send_squares(0, 0, total)
    spread_relayed(1)
    arrived(1)
    left_stage(0, 0)
    push(3)
    total = first_part(1, near_u)
    total = total + first_part(1, far_u)
    send_squares(0, 1, total)
    spread(2)

    def layer(l, carry):
        left_stage(l, 1)
        spread_relayed(2 * l + 2)
        push(2 * l + 4)
        arrived(2 * l + 2)
        next_stage(l, 0)
        spread(2 * l + 3)
        next_stage(l, 1)
        spread_relayed(2 * l + 3)
        push(2 * l + 5)
        arrived(2 * l + 3)
        left_stage(l + 1, 0)
        spread(2 * l + 4)
        return carry

    lax.fori_loop(0, layers - 2, layer, 0)
    left_stage(layers - 2, 1)
    spread_relayed(steps - 2)
    spread(steps - 1)
    arrived(steps - 2)
    next_stage(layers - 2, 0)
    spread_relayed(steps - 1)
    arrived(steps - 1)
    left_stage(layers - 1, 0, True)
    next_stage(layers - 2, 1)
    last_stage(layers - 1, 0)
    left_stage(layers - 1, 1, True)
    last_stage(layers - 1, 1)

    for step in range(steps):
        @pl.when(c == (step // 2) % 2)
        def _():
            share_copy(step, step % 2, 1).wait_send()

        for s in range(cuts):
            for i in range(2):
                push_copy(step, i, s).wait_send()
            for i in range(1, 4):
                forward_copy(step, planes[i], s).wait_send()

            @pl.when(inner_plane)
            def _():
                for i in range(2):
                    relay_copy(step, i, s).wait_send()

    for i, dc in others:
        if i or dc:
            gain_copy(i, dc).wait_send()
            for h in range(2):
                token_copy(h, i, dc).wait_send()
                out_copy(h, i, dc).wait_send()
    for h in range(2):
        for zz in range(hi):
            for cc in range(2):
                first = (2 * zz + h) * few
                piece = out_ref.at[first:first + few, cc * wide:(cc + 1) * wide]
                pltpu.make_async_copy(piece, piece, orecv.at[h, zz, cc]).wait()


def quad_body(tokens, gains, right_factors, left_factors):
    f32 = jnp.float32
    hi = lax.axis_size("hi")
    rounds, here, size = right_factors.shape[1:4]
    layers = 2 * rounds
    rows = here * size // 2
    few = tokens.shape[0] // hi
    cuts = 2
    rates = gains[0].reshape(rounds, 2, here // 2, size)
    rights = right_factors[0].swapaxes(-1, -2).reshape(rounds, here * size, size)
    lefts = left_factors[0].swapaxes(-1, -2).reshape(rounds, here * size, size)
    dma = pltpu.SemaphoreType.DMA
    anywhere = pl.BlockSpec(memory_space=pl.ANY)
    return pl.pallas_call(
        functools.partial(layers_kernel, hi, layers),
        out_shape=jax.ShapeDtypeStruct(tokens.shape, f32),
        in_specs=[anywhere] * 4,
        out_specs=anywhere,
        scratch_shapes=[
            pltpu.VMEM((2 * layers, hi, rows, 128), f32),
            pltpu.VMEM((2, hi * 4, 128, 128), f32),
            pltpu.VMEM((2, hi * 4, 128, 128), f32),
            pltpu.VMEM((2, 2, 4, hi, 8, 8, 128), f32),
            pltpu.VMEM((2, hi, 2, 4, 8, 8, 128), f32),
            pltpu.VMEM((2, hi, 4, 8, 2, 8, 128), f32),
            pltpu.VMEM((2, hi, 4, 8, 2, 8, 128), f32),
            pltpu.VMEM((layers, 2, 4, 8, 128), f32),
            pltpu.VMEM((2, hi, few, rows), f32),
            pltpu.VMEM((2, rounds, 128, 128), f32),
            pltpu.VMEM((layers, hi * 4, 128, 128), f32),
            dma((2, hi, 2)),
            dma((2, hi, 2)),
            dma((hi, 2)),
            dma((hi, 2)),
            dma((2, hi, 2)),
            dma((2, hi, 2)),
            dma((2 * layers,)),
            dma((2 * layers, 2, cuts)),
            dma((2 * layers, hi, cuts)),
            dma((2 * layers, 2, cuts)),
            dma((2 * layers, hi, cuts)),
            dma((2 * layers, hi, cuts)),
            dma((layers, 2, 4)),
            dma((layers, 2, 4)),
            dma((2, 2, 4)),
            dma((2, 2, 4)),
            dma((2, hi, 4)),
            dma((2, hi, 4)),
            dma((2, 2, 4)),
            dma((2, 2, 4)),
        ],
        compiler_params=pltpu.CompilerParams(
            collective_id=0, has_side_effects=True, vmem_limit_bytes=58 * 2**20
        ),
    )(tokens, rates, rights, lefts)


def solution(mesh):
    groups, segments, devices = (mesh.shape[a] for a in ("groups", "segment", "block"))
    if (groups, segments, devices) == (2, 2, 8):
        finer = Mesh(mesh.devices.reshape(2, 2, 4, 2), ("groups", "segment", "hi", "lo"))
        block, chosen = ("hi", "lo"), quad_body
    else:
        finer, block, chosen = mesh, "block", body
    placed = (
        P(("groups", "segment"), block),
        P("segment", None, block),
        P("segment", None, block, None, None),
        P("segment", None, block, None, None),
    )
    return jax.shard_map(
        chosen,
        mesh=finer,
        in_specs=placed,
        out_specs=P(("groups", "segment"), block),
        check_vma=False,
    )
```

```python
import functools

import jax
import jax.numpy as jnp
from jax import lax
from jax.experimental import pallas as pl
from jax.experimental.pallas import tpu as pltpu
from jax.sharding import Mesh, PartitionSpec as P

D = 16384


epsilon = 1e-06
exact = lax.Precision.HIGH


def shifted(block, axis, distance):
    devices = range(lax.axis_size(axis))
    route = [((i - distance) % len(devices), i) for i in devices]
    return lax.ppermute(block, axis, route)


def apply_layer(current, gain_row, right_part, left_part):
    blocks_here = right_part.shape[0]
    block_size = right_part.shape[1]
    width_here, token_count = current.shape
    partial_squares = jnp.sum(current * current, axis=0)
    devices = lax.axis_size("block")
    copies = jnp.broadcast_to(partial_squares, (devices, token_count))
    sum_squares = lax.all_to_all(copies, "block", 0, 0, tiled=True).sum(axis=0)
    normed = current * lax.rsqrt(sum_squares / D + epsilon)[None, :] * gain_row[:, None]
    inner = jnp.einsum(
        "bit,bij->bjt",
        normed.reshape(blocks_here, block_size, token_count),
        right_part,
        precision=exact,
    )
    combined = jnp.einsum(
        "bjt,jbc->cjt",
        lax.all_to_all(inner, "block", split_axis=1, concat_axis=0, tiled=True),
        left_part,
        precision=exact,
    )
    mixed = lax.all_to_all(combined, "block", split_axis=0, concat_axis=1, tiled=True)
    return current + mixed.reshape(width_here, token_count) * jax.nn.silu(normed)


def body(tokens, gains, right_factors, left_factors):
    current = tokens.T
    rounds = right_factors.shape[1]
    segment_index = lax.axis_index("segment")
    own = (gains[0], right_factors[0], left_factors[0])
    other = [[shifted(part[r], "segment", 1) for part in own] for r in range(rounds)]
    for layer_index in range(2 * rounds):
        section, r = layer_index % 2, layer_index // 2
        chosen = [
            jnp.where(segment_index == section, mine[r], theirs)
            for mine, theirs in zip(own, other[r])
        ]
        current = apply_layer(current, *chosen)
    return current.T


MESH = pl.DeviceIdType.MESH


def halves(value):
    high = value.astype(jnp.bfloat16)
    return high, (value - high.astype(jnp.float32)).astype(jnp.bfloat16)


def product(weight, value):
    wh, wl = halves(weight)
    vh, vl = halves(value)
    dot = functools.partial(jnp.dot, preferred_element_type=jnp.float32)
    return dot(wh, vh) + (dot(wh, vl) + dot(wl, vh))


def layers_kernel(
    hi, layers, token_ref, gain_ref, right_ref, left_ref, out_ref,
    W, X, N, S, A, T, M, Q, B, G, P,
    tsend, trecv, gsend, grecv, osend, orecv,
    ssend, psend, wrecv, rsend, fsend, frecv, qsend, qrecv, asend, arecv, msend, mrecv, nsend, nrecv,
):
    x = lax.axis_index("groups")
    c = lax.axis_index("segment")
    z = lax.axis_index("hi")
    y = lax.axis_index("lo")
    here = 2 * y + c
    half = W.shape[2] // 2
    cuts = psend.shape[2]
    steps = 2 * layers
    beside = z + 1 - 2 * (z % 2)
    across = 2 - z // 2
    far = 2 - 2 * (z // 2)
    inner_plane = (z == 1) | (z == 2)
    planes = (z, beside, far, far + 1)
    few, wide = B.shape[2] // 2, B.shape[3]
    near_u, far_u = z // 2, 1 - z // 2
    low = lax.broadcasted_iota(jnp.int32, (128, 128), 1) < 64

    def peer(d):
        return (x, (c + d % 2) % 2, z, (y + d // 2) % 2)

    G[...] = jnp.zeros(G.shape, jnp.float32)
    barrier = pltpu.get_barrier_semaphore()
    greeted = [(x, (c + dc) % 2, (z + dz) % hi, y) for dz in range(hi) for dc in range(2) if dz or dc]
    greeted += [peer(2), peer(3), (1 - x, c, z, y)]
    for device in greeted:
        pl.semaphore_signal(barrier, inc=1, device_id=device, device_id_type=MESH)
    pl.semaphore_wait(barrier, len(greeted))

    def copy_to(src, dst, send, recv, i, dc):
        if i == 0 and dc == 0:
            return pltpu.make_async_copy(src, dst, recv)
        return pltpu.make_async_remote_copy(
            src_ref=src, dst_ref=dst, send_sem=send, recv_sem=recv,
            device_id=(x, (c + dc) % 2, planes[i], y), device_id_type=MESH,
        )

    others = [(i, dc) for i in range(4) for dc in range(2)]

    def token_copy(h, i, dc):
        rows = pl.ds(pl.multiple_of((2 * planes[i] + h) * few, few), few)
        columns = pl.ds(pl.multiple_of((c + dc) % 2 * wide, wide), wide)
        dst = B.at[h, z, pl.ds(pl.multiple_of(c * few, few), few)]
        return copy_to(token_ref.at[rows, columns], dst, tsend.at[h, i, dc], trecv.at[h, z, c], i, dc)

    def gain_copy(i, dc):
        src = gain_ref.at[:, (c + dc) % 2]
        dst = G.at[c, :, pl.ds(pl.multiple_of(z * 8, 8), 8)]
        return copy_to(src, dst, gsend.at[i, dc], grecv.at[z, c], i, dc)

    def out_copy(h, i, dc):
        src = B.at[h, planes[i], pl.ds(pl.multiple_of((c + dc) % 2 * few, few), few)]
        rows = pl.ds(pl.multiple_of((2 * z + h) * few, few), few)
        columns = pl.ds(pl.multiple_of(c * wide, wide), wide)
        return copy_to(src, out_ref.at[rows, columns], osend.at[h, i, dc], orecv.at[h, z, c], i, dc)

    def share_copy(step, f, dc):
        source = (right_ref, left_ref)[f]
        rows = pl.ds(pl.multiple_of((c + dc) % 2 * 2 * half, 2 * half), 2 * half)
        src = source.at[step // 4, rows]
        return copy_to(src, W.at[step, z], ssend.at[step], wrecv.at[step, z, 0], 0, dc)

    def share(step, f):
        @pl.when(c == (step // 2) % 2)
        def _():
            for dc in (1, 0):
                share_copy(step, f, dc).start()

    def piece_at(step, plane, s):
        size = half // cuts
        return W.at[step, plane, pl.ds(pl.multiple_of(x * half + s * size, size), size)]

    def push_copy(step, i, s):
        piece = piece_at(step, z, s)
        return pltpu.make_async_remote_copy(
            src_ref=piece, dst_ref=piece, send_sem=psend.at[step, i, s], recv_sem=wrecv.at[step, z, s],
            device_id=(x, c, (across, beside)[i], y), device_id_type=MESH,
        )

    def push(step):
        pltpu.make_async_copy(W.at[step, z], W.at[step, z], wrecv.at[step, z, 0]).wait()
        for s in range(cuts):
            for i in range(2):
                push_copy(step, i, s).start()

    def forward_copy(step, plane, s):
        piece = piece_at(step, plane, s)
        return pltpu.make_async_remote_copy(
            src_ref=piece, dst_ref=piece,
            send_sem=fsend.at[step, plane, s], recv_sem=frecv.at[step, plane, s],
            device_id=(1 - x, c, z, y), device_id_type=MESH,
        )

    def relay_copy(step, i, s):
        piece = piece_at(step, far + i, s)
        return pltpu.make_async_remote_copy(
            src_ref=piece, dst_ref=piece,
            send_sem=rsend.at[step, i, s], recv_sem=wrecv.at[step, far + i, s],
            device_id=(x, c, beside, y), device_id_type=MESH,
        )

    def piece_wait(step, plane, s):
        piece = piece_at(step, plane, s)
        pltpu.make_async_copy(piece, piece, wrecv.at[step, plane, s]).wait()

    def spread(step):
        for s in range(cuts):
            piece_wait(step, beside, s)
            forward_copy(step, beside, s).start()

            @pl.when(inner_plane)
            def _():
                for i in range(2):
                    piece_wait(step, far + i, s)
                    relay_copy(step, i, s).start()
                    forward_copy(step, far + i, s).start()

    def spread_relayed(step):
        @pl.when(~inner_plane)
        def _():
            for s in range(cuts):
                for i in range(2):
                    piece_wait(step, far + i, s)
                    forward_copy(step, far + i, s).start()

    def arrived_near(step):
        for s in range(cuts):
            forward_copy(step, beside, s).wait_recv()

    def arrived_far(step):
        for s in range(cuts):
            for i in range(2):
                forward_copy(step, far + i, s).wait_recv()

    def arrived(step):
        arrived_near(step)
        arrived_far(step)

    def quad_copy(kind, h, part, d):
        if kind == "q":
            ref = Q.at[part, h, here]
            src, dst, send, recv = ref, ref, qsend.at[part, h, d], qrecv.at[part, h, d]
        else:
            target = 2 * ((y + d // 2) % 2) + (c + d % 2) % 2
            if kind == "a":
                src, dst, send, recv = S.at[h, part, target], A.at[h, :, part, here], asend, arecv
            elif kind == "m":
                src, dst, send, recv = T.at[h, part, target], M.at[h, part, here], msend, mrecv
            else:
                src, dst, send, recv = T.at[h, :, target, :, part], M.at[h, :, here, :, part], nsend, nrecv
            send, recv = send.at[h, part, d], recv.at[h, part, d]
            if d == 0:
                return pltpu.make_async_copy(src, dst, recv)
        return pltpu.make_async_remote_copy(
            src_ref=src, dst_ref=dst, send_sem=send, recv_sem=recv,
            device_id=peer(d), device_id_type=MESH,
        )

    def squares(value):
        return jnp.sum((value * value).reshape(16, 8, 128), axis=0)

    def right_pair(l, h, u, k, value):
        p = u * 8 + k
        v = value * P[l, p]
        N[h, p] = v
        packed = jnp.concatenate([jnp.where(low, v, 0.0), jnp.where(low, 0.0, v)], axis=0)
        weight = jnp.concatenate([W[2 * l, 2 * u + e, k * 128:(k + 1) * 128].T for e in range(2)], axis=1)
        tiles = product(weight, packed).reshape(hi, 4, 8, 128)
        for q in range(4):
            S[h, u, q, :, k] = tiles[:, q]

    def send_inner(h, u):
        for d in (2, 3, 1, 0):
            quad_copy("a", h, u, d).start()

    def send_squares(l, h, total):
        Q[l, h, here] = total
        for d in (2, 3, 1):
            quad_copy("q", h, l, d).start()

    def first_part(h, u):
        total = jnp.zeros((8, 128), jnp.float32)
        for e in range(2):
            for cc in range(2):
                piece = B.at[h, 2 * u + e, :few]
                pltpu.make_async_copy(piece, piece, trecv.at[h, 2 * u + e, cc]).wait()
        for k in range(8):
            columns = slice(k * 128, (k + 1) * 128)
            value = jnp.concatenate([B[h, 2 * u, :, columns], B[h, 2 * u + 1, :, columns]], axis=0).T
            X[h, u * 8 + k] = value
            right_pair(0, h, u, k, value)
            total = total + squares(value)
        send_inner(h, u)
        return total

    def left_stage(l, h, last=False, between=None):
        for part in range(2):
            for d in range(4):
                quad_copy("a", h, part, d).wait()

        def left_chunk(i, carry):
            zj = (2 * near_u + i) % hi
            flat = A.at[h, zj].reshape(2 * 4 * 8 * 8, 128)
            for jj in range(8):
                a = flat[pl.ds(jj, 64, stride=8), :]
                swapped = pltpu.roll(a, 64, 1)
                mask = low[:64]
                al, ah = jnp.where(mask, a, 0.0), jnp.where(mask, 0.0, a)
                sl, sh = jnp.where(mask, swapped, 0.0), jnp.where(mask, 0.0, swapped)
                packed = jnp.concatenate(
                    [al[:32], sl[:32], al[32:], sl[32:], sh[:32], ah[:32], sh[32:], ah[32:]], axis=0
                )
                w = W[2 * l + 1, zj, jj * 128:(jj + 1) * 128].T
                weight = jnp.concatenate(
                    [jnp.concatenate([w[s:s + 32], w[s + 64:s + 96]], axis=0) for s in (0, 32)], axis=1
                )
                tiles = product(weight, packed).reshape(2, 4, 8, 128)
                for q in range(4):
                    T[h, zj, q, jj] = tiles[:, q]
            if not last:
                for d in (2, 3, 1, 0):
                    quad_copy("m", h, zj, d).start()
            return carry

        if between is None:
            lax.fori_loop(0, hi, left_chunk, 0)
        else:
            arrived_near(2 * l + 1)
            lax.fori_loop(0, hi // 2, left_chunk, 0)
            between()
            arrived_far(2 * l + 1)
            lax.fori_loop(hi // 2, hi, left_chunk, 0)
        if last:
            for u in (far_u, near_u):
                for d in (2, 3, 1, 0):
                    quad_copy("n", h, u, d).start()

    def closing(l, h):
        for d in (2, 3, 1):
            quad_copy("q", h, l, d).wait()
        everyone = Q[l, h, 0] + Q[l, h, 1] + Q[l, h, 2] + Q[l, h, 3]
        one = jnp.sum(everyone, axis=0, keepdims=True)
        both = jnp.broadcast_to(one, (8, 128))
        both = both + pltpu.roll(both, 64, 1)
        scale = lax.rsqrt(both[:1] / D + epsilon)
        flat = M.at[h].reshape(128 * 16, 128)

        def close_pair(p):
            normed = N[h, p] * scale
            mixed = flat[pl.ds(p, 128, stride=16), :] * scale
            return X[h, p] + mixed * (normed / (1.0 + jnp.exp(-normed)))

        return close_pair

    def next_stage(l, h, first=False):
        close_pair = closing(l, h)
        for part in range(hi):
            for d in range(4):
                quad_copy("m", h, part, d).wait()

        def part(i, total):
            u = (near_u + i) % 2
            for k in range(8):
                value = close_pair(u * 8 + k)
                X[h, u * 8 + k] = value
                right_pair(l + 1, h, u, k, value)
                total = total + squares(value)
            send_inner(h, u)
            return total

        total = jnp.zeros((8, 128), jnp.float32)
        if first:
            arrived_near(2 * l + 2)
            total = lax.fori_loop(0, 1, part, total)
            arrived_far(2 * l + 2)
            total = lax.fori_loop(1, 2, part, total)
        else:
            total = lax.fori_loop(0, 2, part, total)
        send_squares(l + 1, h, total)

    def last_stage(l, h):
        close_pair = closing(l, h)
        for near in (0, 1):
            u = (far_u, near_u)[near]
            for d in range(4):
                quad_copy("n", h, u, d).wait()
            for k in range(8):
                columns = slice(k * 128, (k + 1) * 128)
                value = close_pair(u * 8 + k).T
                B[h, 2 * u, :, columns] = value[:2 * few]
                B[h, 2 * u + 1, :, columns] = value[2 * few:]
            for i in ((2, 3), (1, 0))[near]:
                for dc in range(2):
                    out_copy(h, i, dc).start()

    for i, dc in others:
        gain_copy(i, dc).start()
    for step in range(4):
        share(step, step % 2)
    for i, dc in others[:4]:
        token_copy(0, i, dc).start()
    push(0)
    push(1)
    for i, dc in others[4:]:
        token_copy(0, i, dc).start()
    for step in range(4, steps):
        share(step, step % 2)
    for zz in range(hi):
        for cc in range(2):
            piece = G.at[cc, :, zz * 8:(zz + 1) * 8]
            pltpu.make_async_copy(piece, piece, grecv.at[zz, cc]).wait()

    def pack_gains(l, carry):
        columns = G[l % 2, l // 2].T
        for u in range(2):
            for k in range(8):
                first, second = u * 16 + k, u * 16 + 8 + k
                P[l, u * 8 + k] = jnp.where(low, columns[:, first:first + 1], columns[:, second:second + 1])
        return carry

    lax.fori_loop(0, layers, pack_gains, 0)
    spread(0)
    spread(1)
    for i, dc in others:
        token_copy(1, i, dc).start()
    push(2)
    arrived_near(0)
    total = first_part(0, near_u)
    spread_relayed(0)
    arrived_far(0)
    total = total + first_part(0, far_u)
    send_squares(0, 0, total)
    left_stage(0, 0, between=lambda: spread_relayed(1))
    push(3)
    total = first_part(1, near_u)
    total = total + first_part(1, far_u)
    send_squares(0, 1, total)
    spread(2)

    def layer(l, carry):
        left_stage(l, 1)
        spread_relayed(2 * l + 2)
        push(2 * l + 4)
        next_stage(l, 0, True)
        spread(2 * l + 3)
        next_stage(l, 1)
        spread_relayed(2 * l + 3)
        push(2 * l + 5)
        left_stage(l + 1, 0, between=lambda: None)
        spread(2 * l + 4)
        return carry

    lax.fori_loop(0, layers - 2, layer, 0)
    left_stage(layers - 2, 1)
    spread_relayed(steps - 2)
    spread(steps - 1)
    next_stage(layers - 2, 0, True)
    spread_relayed(steps - 1)
    left_stage(layers - 1, 0, True, lambda: None)
    next_stage(layers - 2, 1)
    last_stage(layers - 1, 0)
    left_stage(layers - 1, 1, True)
    last_stage(layers - 1, 1)

    for step in range(steps):
        @pl.when(c == (step // 2) % 2)
        def _():
            share_copy(step, step % 2, 1).wait_send()

        for s in range(cuts):
            for i in range(2):
                push_copy(step, i, s).wait_send()
            for i in range(1, 4):
                forward_copy(step, planes[i], s).wait_send()

            @pl.when(inner_plane)
            def _():
                for i in range(2):
                    relay_copy(step, i, s).wait_send()

    for i, dc in others:
        if i or dc:
            gain_copy(i, dc).wait_send()
            for h in range(2):
                token_copy(h, i, dc).wait_send()
                out_copy(h, i, dc).wait_send()
    for h in range(2):
        for zz in range(hi):
            for cc in range(2):
                first = (2 * zz + h) * few
                piece = out_ref.at[first:first + few, cc * wide:(cc + 1) * wide]
                pltpu.make_async_copy(piece, piece, orecv.at[h, zz, cc]).wait()


def quad_body(tokens, gains, right_factors, left_factors):
    f32 = jnp.float32
    hi = lax.axis_size("hi")
    rounds, here, size = right_factors.shape[1:4]
    layers = 2 * rounds
    rows = here * size // 2
    few = tokens.shape[0] // hi
    cuts = 2
    rates = gains[0].reshape(rounds, 2, here // 2, size)
    rights = right_factors[0].reshape(rounds, here * size, size)
    lefts = left_factors[0].reshape(rounds, here * size, size)
    dma = pltpu.SemaphoreType.DMA
    anywhere = pl.BlockSpec(memory_space=pl.ANY)
    return pl.pallas_call(
        functools.partial(layers_kernel, hi, layers),
        out_shape=jax.ShapeDtypeStruct(tokens.shape, f32),
        in_specs=[anywhere] * 4,
        out_specs=anywhere,
        scratch_shapes=[
            pltpu.VMEM((2 * layers, hi, rows, 128), f32),
            pltpu.VMEM((2, hi * 4, 128, 128), f32),
            pltpu.VMEM((2, hi * 4, 128, 128), f32),
            pltpu.VMEM((2, 2, 4, hi, 8, 8, 128), f32),
            pltpu.VMEM((2, hi, 2, 4, 8, 8, 128), f32),
            pltpu.VMEM((2, hi, 4, 8, 2, 8, 128), f32),
            pltpu.VMEM((2, hi, 4, 8, 2, 8, 128), f32),
            pltpu.VMEM((layers, 2, 4, 8, 128), f32),
            pltpu.VMEM((2, hi, few, rows), f32),
            pltpu.VMEM((2, rounds, 128, 128), f32),
            pltpu.VMEM((layers, hi * 4, 128, 128), f32),
            dma((2, hi, 2)),
            dma((2, hi, 2)),
            dma((hi, 2)),
            dma((hi, 2)),
            dma((2, hi, 2)),
            dma((2, hi, 2)),
            dma((2 * layers,)),
            dma((2 * layers, 2, cuts)),
            dma((2 * layers, hi, cuts)),
            dma((2 * layers, 2, cuts)),
            dma((2 * layers, hi, cuts)),
            dma((2 * layers, hi, cuts)),
            dma((layers, 2, 4)),
            dma((layers, 2, 4)),
            dma((2, 2, 4)),
            dma((2, 2, 4)),
            dma((2, hi, 4)),
            dma((2, hi, 4)),
            dma((2, 2, 4)),
            dma((2, 2, 4)),
        ],
        compiler_params=pltpu.CompilerParams(
            collective_id=0, has_side_effects=True, vmem_limit_bytes=58 * 2**20
        ),
    )(tokens, rates, rights, lefts)


def solution(mesh):
    groups, segments, devices = (mesh.shape[a] for a in ("groups", "segment", "block"))
    if (groups, segments, devices) == (2, 2, 8):
        finer = Mesh(mesh.devices.reshape(2, 2, 4, 2), ("groups", "segment", "hi", "lo"))
        block, chosen = ("hi", "lo"), quad_body
    else:
        finer, block, chosen = mesh, "block", body
    placed = (
        P(("groups", "segment"), block),
        P("segment", None, block),
        P("segment", None, block, None, None),
        P("segment", None, block, None, None),
    )
    return jax.shard_map(
        chosen,
        mesh=finer,
        in_specs=placed,
        out_specs=P(("groups", "segment"), block),
        check_vma=False,
    )
```

```python
import functools

import jax
import jax.numpy as jnp
from jax import lax
from jax.experimental import pallas as pl
from jax.experimental.pallas import tpu as pltpu
from jax.sharding import Mesh, PartitionSpec as P

D = 16384


epsilon = 1e-06
exact = lax.Precision.HIGH


def shifted(block, axis, distance):
    devices = range(lax.axis_size(axis))
    route = [((i - distance) % len(devices), i) for i in devices]
    return lax.ppermute(block, axis, route)


def apply_layer(current, gain_row, right_part, left_part):
    blocks_here = right_part.shape[0]
    block_size = right_part.shape[1]
    width_here, token_count = current.shape
    partial_squares = jnp.sum(current * current, axis=0)
    devices = lax.axis_size("block")
    copies = jnp.broadcast_to(partial_squares, (devices, token_count))
    sum_squares = lax.all_to_all(copies, "block", 0, 0, tiled=True).sum(axis=0)
    normed = current * lax.rsqrt(sum_squares / D + epsilon)[None, :] * gain_row[:, None]
    inner = jnp.einsum(
        "bit,bij->bjt",
        normed.reshape(blocks_here, block_size, token_count),
        right_part,
        precision=exact,
    )
    combined = jnp.einsum(
        "bjt,jbc->cjt",
        lax.all_to_all(inner, "block", split_axis=1, concat_axis=0, tiled=True),
        left_part,
        precision=exact,
    )
    mixed = lax.all_to_all(combined, "block", split_axis=0, concat_axis=1, tiled=True)
    return current + mixed.reshape(width_here, token_count) * jax.nn.silu(normed)


def body(tokens, gains, right_factors, left_factors):
    current = tokens.T
    rounds = right_factors.shape[1]
    segment_index = lax.axis_index("segment")
    own = (gains[0], right_factors[0], left_factors[0])
    other = [[shifted(part[r], "segment", 1) for part in own] for r in range(rounds)]
    for layer_index in range(2 * rounds):
        section, r = layer_index % 2, layer_index // 2
        chosen = [
            jnp.where(segment_index == section, mine[r], theirs)
            for mine, theirs in zip(own, other[r])
        ]
        current = apply_layer(current, *chosen)
    return current.T


MESH = pl.DeviceIdType.MESH


def halves(value):
    high = value.astype(jnp.bfloat16)
    return high, (value - high.astype(jnp.float32)).astype(jnp.bfloat16)


def product(weight, value):
    wh, wl = halves(weight)
    vh, vl = halves(value)
    dot = functools.partial(jnp.dot, preferred_element_type=jnp.float32)
    return dot(wh, vh) + (dot(wh, vl) + dot(wl, vh))


def layers_kernel(
    hi, layers, token_ref, gain_ref, right_ref, left_ref, out_ref,
    W, X, N, S, A, T, M, Q, B, G, P,
    tsend, trecv, gsend, grecv, osend, orecv,
    ssend, psend, wrecv, rsend, fsend, frecv, qsend, qrecv, asend, arecv, msend, mrecv, nsend, nrecv,
):
    x = lax.axis_index("groups")
    c = lax.axis_index("segment")
    z = lax.axis_index("hi")
    y = lax.axis_index("lo")
    here = 2 * y + c
    half = W.shape[2] // 2
    cuts = psend.shape[2]
    steps = 2 * layers
    beside = z + 1 - 2 * (z % 2)
    across = 2 - z // 2
    far = 2 - 2 * (z // 2)
    inner_plane = (z == 1) | (z == 2)
    planes = (z, beside, far, far + 1)
    few, wide = B.shape[2] // 2, B.shape[3]
    near_u, far_u = z // 2, 1 - z // 2
    low = lax.broadcasted_iota(jnp.int32, (128, 128), 1) < 64

    def peer(d):
        return (x, (c + d % 2) % 2, z, (y + d // 2) % 2)

    G[...] = jnp.zeros(G.shape, jnp.float32)
    barrier = pltpu.get_barrier_semaphore()
    greeted = [(x, (c + dc) % 2, (z + dz) % hi, y) for dz in range(hi) for dc in range(2) if dz or dc]
    greeted += [peer(2), peer(3), (1 - x, c, z, y)]
    for device in greeted:
        pl.semaphore_signal(barrier, inc=1, device_id=device, device_id_type=MESH)
    pl.semaphore_wait(barrier, len(greeted))

    def copy_to(src, dst, send, recv, i, dc):
        if i == 0 and dc == 0:
            return pltpu.make_async_copy(src, dst, recv)
        return pltpu.make_async_remote_copy(
            src_ref=src, dst_ref=dst, send_sem=send, recv_sem=recv,
            device_id=(x, (c + dc) % 2, planes[i], y), device_id_type=MESH,
        )

    others = [(i, dc) for i in range(4) for dc in range(2)]

    def token_copy(h, i, dc):
        rows = pl.ds(pl.multiple_of((2 * planes[i] + h) * few, few), few)
        columns = pl.ds(pl.multiple_of((c + dc) % 2 * wide, wide), wide)
        dst = B.at[h, z, pl.ds(pl.multiple_of(c * few, few), few)]
        return copy_to(token_ref.at[rows, columns], dst, tsend.at[h, i, dc], trecv.at[h, z, c], i, dc)

    def gain_copy(i, dc):
        src = gain_ref.at[:, (c + dc) % 2]
        dst = G.at[c, :, pl.ds(pl.multiple_of(z * 8, 8), 8)]
        return copy_to(src, dst, gsend.at[i, dc], grecv.at[z, c], i, dc)

    def out_copy(h, i, dc):
        src = B.at[h, planes[i], pl.ds(pl.multiple_of((c + dc) % 2 * few, few), few)]
        rows = pl.ds(pl.multiple_of((2 * z + h) * few, few), few)
        columns = pl.ds(pl.multiple_of(c * wide, wide), wide)
        return copy_to(src, out_ref.at[rows, columns], osend.at[h, i, dc], orecv.at[h, z, c], i, dc)

    def share_copy(step, f, dc):
        source = (right_ref, left_ref)[f]
        rows = pl.ds(pl.multiple_of((c + dc) % 2 * 2 * half, 2 * half), 2 * half)
        src = source.at[step // 4, rows]
        return copy_to(src, W.at[step, z], ssend.at[step], wrecv.at[step, z, 0], 0, dc)

    def share(step, f):
        @pl.when(c == (step // 2) % 2)
        def _():
            for dc in (1, 0):
                share_copy(step, f, dc).start()

    def piece_at(step, plane, s):
        size = half // cuts
        return W.at[step, plane, pl.ds(pl.multiple_of(x * half + s * size, size), size)]

    def push_copy(step, i, s):
        piece = piece_at(step, z, s)
        return pltpu.make_async_remote_copy(
            src_ref=piece, dst_ref=piece, send_sem=psend.at[step, i, s], recv_sem=wrecv.at[step, z, s],
            device_id=(x, c, (across, beside)[i], y), device_id_type=MESH,
        )

    def push(step):
        pltpu.make_async_copy(W.at[step, z], W.at[step, z], wrecv.at[step, z, 0]).wait()
        for s in range(cuts):
            for i in range(2):
                push_copy(step, i, s).start()

    def forward_copy(step, plane, s):
        piece = piece_at(step, plane, s)
        return pltpu.make_async_remote_copy(
            src_ref=piece, dst_ref=piece,
            send_sem=fsend.at[step, plane, s], recv_sem=frecv.at[step, plane, s],
            device_id=(1 - x, c, z, y), device_id_type=MESH,
        )

    def relay_copy(step, i, s):
        piece = piece_at(step, far + i, s)
        return pltpu.make_async_remote_copy(
            src_ref=piece, dst_ref=piece,
            send_sem=rsend.at[step, i, s], recv_sem=wrecv.at[step, far + i, s],
            device_id=(x, c, beside, y), device_id_type=MESH,
        )

    def piece_wait(step, plane, s):
        piece = piece_at(step, plane, s)
        pltpu.make_async_copy(piece, piece, wrecv.at[step, plane, s]).wait()

    def spread(step):
        for s in range(cuts):
            piece_wait(step, beside, s)
            forward_copy(step, beside, s).start()

            @pl.when(inner_plane)
            def _():
                for i in range(2):
                    piece_wait(step, far + i, s)
                    relay_copy(step, i, s).start()
                    forward_copy(step, far + i, s).start()

    def spread_relayed(step):
        @pl.when(~inner_plane)
        def _():
            for s in range(cuts):
                for i in range(2):
                    piece_wait(step, far + i, s)
                    forward_copy(step, far + i, s).start()

    def arrived_near(step):
        for s in range(cuts):
            forward_copy(step, beside, s).wait_recv()

    def arrived_far(step):
        for s in range(cuts):
            for i in range(2):
                forward_copy(step, far + i, s).wait_recv()

    def arrived(step):
        arrived_near(step)
        arrived_far(step)

    def quad_copy(kind, h, part, d):
        if kind == "q":
            ref = Q.at[part, h, here]
            src, dst, send, recv = ref, ref, qsend.at[part, h, d], qrecv.at[part, h, d]
        else:
            target = 2 * ((y + d // 2) % 2) + (c + d % 2) % 2
            if kind == "a":
                src, dst, send, recv = S.at[h, part, target], A.at[h, :, part, here], asend, arecv
            elif kind == "m":
                src, dst, send, recv = T.at[h, part, target], M.at[h, part, here], msend, mrecv
            else:
                src, dst, send, recv = T.at[h, :, target, :, part], M.at[h, :, here, :, part], nsend, nrecv
            send, recv = send.at[h, part, d], recv.at[h, part, d]
            if d == 0:
                return pltpu.make_async_copy(src, dst, recv)
        return pltpu.make_async_remote_copy(
            src_ref=src, dst_ref=dst, send_sem=send, recv_sem=recv,
            device_id=peer(d), device_id_type=MESH,
        )

    def squares(value):
        return jnp.sum((value * value).reshape(16, 8, 128), axis=0)

    def right_pair(l, h, u, k, value):
        p = u * 8 + k
        v = value * P[l, p]
        N[h, p] = v
        packed = jnp.concatenate([jnp.where(low, v, 0.0), jnp.where(low, 0.0, v)], axis=0)
        weight = jnp.concatenate([W[2 * l, 2 * u + e, k * 128:(k + 1) * 128].T for e in range(2)], axis=1)
        tiles = product(weight, packed).reshape(hi, 4, 8, 128)
        for q in range(4):
            S[h, u, q, :, k] = tiles[:, q]

    def send_inner(h, u):
        for d in (2, 3, 1, 0):
            quad_copy("a", h, u, d).start()

    def send_squares(l, h, total):
        Q[l, h, here] = total
        for d in (2, 3, 1):
            quad_copy("q", h, l, d).start()

    def first_part(h, u):
        total = jnp.zeros((8, 128), jnp.float32)
        for e in range(2):
            for cc in range(2):
                piece = B.at[h, 2 * u + e, :few]
                pltpu.make_async_copy(piece, piece, trecv.at[h, 2 * u + e, cc]).wait()
        for k in range(8):
            columns = slice(k * 128, (k + 1) * 128)
            value = jnp.concatenate([B[h, 2 * u, :, columns], B[h, 2 * u + 1, :, columns]], axis=0).T
            X[h, u * 8 + k] = value
            right_pair(0, h, u, k, value)
            total = total + squares(value)
        send_inner(h, u)
        return total

    def left_stage(l, h, last=False, between=None):
        for part in range(2):
            for d in range(4):
                quad_copy("a", h, part, d).wait()

        def left_chunk(i, carry):
            zj = (2 * near_u + i) % hi
            flat = A.at[h, zj].reshape(2 * 4 * 8 * 8, 128)
            for jj in range(8):
                a = flat[pl.ds(jj, 64, stride=8), :]
                swapped = pltpu.roll(a, 64, 1)
                mask = low[:64]
                al, ah = jnp.where(mask, a, 0.0), jnp.where(mask, 0.0, a)
                sl, sh = jnp.where(mask, swapped, 0.0), jnp.where(mask, 0.0, swapped)
                packed = jnp.concatenate(
                    [al[:32], sl[:32], al[32:], sl[32:], sh[:32], ah[:32], sh[32:], ah[32:]], axis=0
                )
                w = W[2 * l + 1, zj, jj * 128:(jj + 1) * 128].T
                weight = jnp.concatenate(
                    [jnp.concatenate([w[s:s + 32], w[s + 64:s + 96]], axis=0) for s in (0, 32)], axis=1
                )
                tiles = product(weight, packed).reshape(2, 4, 8, 128)
                for q in range(4):
                    T[h, zj, q, jj] = tiles[:, q]
            if not last:
                for d in (2, 3, 1, 0):
                    quad_copy("m", h, zj, d).start()
            return carry

        if between is None:
            lax.fori_loop(0, hi, left_chunk, 0)
        else:
            arrived_near(2 * l + 1)
            lax.fori_loop(0, hi // 2, left_chunk, 0)
            between()
            arrived_far(2 * l + 1)
            lax.fori_loop(hi // 2, hi, left_chunk, 0)

    def send_half(h, u):
        for d in (2, 3, 1, 0):
            quad_copy("n", h, u, d).start()

    def closing(l, h):
        for d in (2, 3, 1):
            quad_copy("q", h, l, d).wait()
        everyone = Q[l, h, 0] + Q[l, h, 1] + Q[l, h, 2] + Q[l, h, 3]
        one = jnp.sum(everyone, axis=0, keepdims=True)
        both = jnp.broadcast_to(one, (8, 128))
        both = both + pltpu.roll(both, 64, 1)
        scale = lax.rsqrt(both[:1] / D + epsilon)
        flat = M.at[h].reshape(128 * 16, 128)

        def close_pair(p):
            normed = N[h, p] * scale
            mixed = flat[pl.ds(p, 128, stride=16), :] * scale
            return X[h, p] + mixed * (normed / (1.0 + jnp.exp(-normed)))

        return close_pair

    def next_stage(l, h, first=False):
        close_pair = closing(l, h)
        for part in range(hi):
            for d in range(4):
                quad_copy("m", h, part, d).wait()

        def part(i, total):
            u = (near_u + i) % 2
            for k in range(8):
                value = close_pair(u * 8 + k)
                X[h, u * 8 + k] = value
                right_pair(l + 1, h, u, k, value)
                total = total + squares(value)
            send_inner(h, u)
            return total

        total = jnp.zeros((8, 128), jnp.float32)
        if first:
            arrived_near(2 * l + 2)
            total = lax.fori_loop(0, 1, part, total)
            arrived_far(2 * l + 2)
            total = lax.fori_loop(1, 2, part, total)
        else:
            total = lax.fori_loop(0, 2, part, total)
        send_squares(l + 1, h, total)

    def last_half(close_pair, h, near):
        u = (far_u, near_u)[near]
        for d in range(4):
            quad_copy("n", h, u, d).wait()
        for k in range(8):
            columns = slice(k * 128, (k + 1) * 128)
            value = close_pair(u * 8 + k).T
            B[h, 2 * u, :, columns] = value[:2 * few]
            B[h, 2 * u + 1, :, columns] = value[2 * few:]
        for i in ((2, 3), (1, 0))[near]:
            for dc in range(2):
                out_copy(h, i, dc).start()

    for i, dc in others:
        gain_copy(i, dc).start()
    for step in range(4):
        share(step, step % 2)
    for i, dc in others[:4]:
        token_copy(0, i, dc).start()
    push(0)
    push(1)
    for i, dc in others[:4]:
        token_copy(1, i, dc).start()
    for i, dc in others[4:]:
        token_copy(0, i, dc).start()
    for step in range(4, steps):
        share(step, step % 2)
    for zz in range(hi):
        for cc in range(2):
            piece = G.at[cc, :, zz * 8:(zz + 1) * 8]
            pltpu.make_async_copy(piece, piece, grecv.at[zz, cc]).wait()

    def pack_gains(l, carry):
        columns = G[l % 2, l // 2].T
        for u in range(2):
            for k in range(8):
                first, second = u * 16 + k, u * 16 + 8 + k
                P[l, u * 8 + k] = jnp.where(low, columns[:, first:first + 1], columns[:, second:second + 1])
        return carry

    lax.fori_loop(0, layers, pack_gains, 0)
    spread(0)
    spread(1)
    for i, dc in others[4:]:
        token_copy(1, i, dc).start()
    push(2)
    arrived_near(0)
    total = first_part(0, near_u)
    spread_relayed(0)
    arrived_far(0)
    total = total + first_part(0, far_u)
    send_squares(0, 0, total)
    left_stage(0, 0, between=lambda: spread_relayed(1))
    push(3)
    total = first_part(1, near_u)
    total = total + first_part(1, far_u)
    send_squares(0, 1, total)
    spread(2)

    def layer(l, carry):
        left_stage(l, 1)
        spread_relayed(2 * l + 2)
        push(2 * l + 4)
        next_stage(l, 0, True)
        spread(2 * l + 3)
        next_stage(l, 1)
        spread_relayed(2 * l + 3)
        push(2 * l + 5)
        left_stage(l + 1, 0, between=lambda: None)
        spread(2 * l + 4)
        return carry

    lax.fori_loop(0, layers - 2, layer, 0)
    left_stage(layers - 2, 1)
    spread_relayed(steps - 2)
    spread(steps - 1)
    next_stage(layers - 2, 0, True)
    spread_relayed(steps - 1)
    left_stage(layers - 1, 0, True, lambda: None)
    send_half(0, far_u)
    next_stage(layers - 2, 1)
    close_first = closing(layers - 1, 0)
    last_half(close_first, 0, 0)
    left_stage(layers - 1, 1, True)
    send_half(1, far_u)
    send_half(0, near_u)
    send_half(1, near_u)
    close_second = closing(layers - 1, 1)
    last_half(close_second, 1, 0)
    last_half(close_first, 0, 1)
    last_half(close_second, 1, 1)

    for step in range(steps):
        @pl.when(c == (step // 2) % 2)
        def _():
            share_copy(step, step % 2, 1).wait_send()

        for s in range(cuts):
            for i in range(2):
                push_copy(step, i, s).wait_send()
            for i in range(1, 4):
                forward_copy(step, planes[i], s).wait_send()

            @pl.when(inner_plane)
            def _():
                for i in range(2):
                    relay_copy(step, i, s).wait_send()

    for i, dc in others:
        if i or dc:
            gain_copy(i, dc).wait_send()
            for h in range(2):
                token_copy(h, i, dc).wait_send()
                out_copy(h, i, dc).wait_send()
    for h in range(2):
        for zz in range(hi):
            for cc in range(2):
                first = (2 * zz + h) * few
                piece = out_ref.at[first:first + few, cc * wide:(cc + 1) * wide]
                pltpu.make_async_copy(piece, piece, orecv.at[h, zz, cc]).wait()


def quad_body(tokens, gains, right_factors, left_factors):
    f32 = jnp.float32
    hi = lax.axis_size("hi")
    rounds, here, size = right_factors.shape[1:4]
    layers = 2 * rounds
    rows = here * size // 2
    few = tokens.shape[0] // hi
    cuts = 2
    rates = gains[0].reshape(rounds, 2, here // 2, size)
    rights = right_factors[0].reshape(rounds, here * size, size)
    lefts = left_factors[0].reshape(rounds, here * size, size)
    dma = pltpu.SemaphoreType.DMA
    anywhere = pl.BlockSpec(memory_space=pl.ANY)
    return pl.pallas_call(
        functools.partial(layers_kernel, hi, layers),
        out_shape=jax.ShapeDtypeStruct(tokens.shape, f32),
        in_specs=[anywhere] * 4,
        out_specs=anywhere,
        scratch_shapes=[
            pltpu.VMEM((2 * layers, hi, rows, 128), f32),
            pltpu.VMEM((2, hi * 4, 128, 128), f32),
            pltpu.VMEM((2, hi * 4, 128, 128), f32),
            pltpu.VMEM((2, 2, 4, hi, 8, 8, 128), f32),
            pltpu.VMEM((2, hi, 2, 4, 8, 8, 128), f32),
            pltpu.VMEM((2, hi, 4, 8, 2, 8, 128), f32),
            pltpu.VMEM((2, hi, 4, 8, 2, 8, 128), f32),
            pltpu.VMEM((layers, 2, 4, 8, 128), f32),
            pltpu.VMEM((2, hi, few, rows), f32),
            pltpu.VMEM((2, rounds, 128, 128), f32),
            pltpu.VMEM((layers, hi * 4, 128, 128), f32),
            dma((2, hi, 2)),
            dma((2, hi, 2)),
            dma((hi, 2)),
            dma((hi, 2)),
            dma((2, hi, 2)),
            dma((2, hi, 2)),
            dma((2 * layers,)),
            dma((2 * layers, 2, cuts)),
            dma((2 * layers, hi, cuts)),
            dma((2 * layers, 2, cuts)),
            dma((2 * layers, hi, cuts)),
            dma((2 * layers, hi, cuts)),
            dma((layers, 2, 4)),
            dma((layers, 2, 4)),
            dma((2, 2, 4)),
            dma((2, 2, 4)),
            dma((2, hi, 4)),
            dma((2, hi, 4)),
            dma((2, 2, 4)),
            dma((2, 2, 4)),
        ],
        compiler_params=pltpu.CompilerParams(
            collective_id=0, has_side_effects=True, vmem_limit_bytes=58 * 2**20
        ),
    )(tokens, rates, rights, lefts)


def solution(mesh):
    groups, segments, devices = (mesh.shape[a] for a in ("groups", "segment", "block"))
    if (groups, segments, devices) == (2, 2, 8):
        finer = Mesh(mesh.devices.reshape(2, 2, 4, 2), ("groups", "segment", "hi", "lo"))
        block, chosen = ("hi", "lo"), quad_body
    else:
        finer, block, chosen = mesh, "block", body
    placed = (
        P(("groups", "segment"), block),
        P("segment", None, block),
        P("segment", None, block, None, None),
        P("segment", None, block, None, None),
    )
    return jax.shard_map(
        chosen,
        mesh=finer,
        in_specs=placed,
        out_specs=P(("groups", "segment"), block),
        check_vma=False,
    )
```
